128 devices in a mesh: seq: 32 (over y, z, core), chan: 4 (over x).
Axes of the slice: x: 4, y: 4, z: 4, core: 2. Of those that a mesh axis runs over, the one named last changes fastest.
Arguments:
- tokens: bfloat16 [16384, 4096], P('seq', 'chan'), may hold values from -6 to 6
- in_weight: bfloat16 [4096, 3, 2048], P(None, None, 'chan'), may hold values from -0.09375 to 0.09375
- short_weight: float32 [3, 3, 2048], P(None, None, 'chan'), may hold values from -3 to 3
- filter_taps: float32 [16384, 2048], P('seq', 'chan'), may hold values from -1.1 to 1.1
- skip_gain: float32 [2048], P('chan'), may hold values from -3 to 3
Outputs:
- hyena_out: bfloat16 [16384, 2048], P('seq', 'chan')
The draws below stay inside these ranges and needn't reach their ends.
All inputs are finite; a program needn't handle non-finite values.
Results may differ from the reference program's by a relative error of at most 0.012.
Values may be sent and summed in bfloat16 or wider, within the bound.
A program may use at most 128 MiB of HBM per device.

```python
import math
import jax
import jax.numpy as jnp
from jax import lax

D = 4096
CH = 2048
LENGTH = 16384


def draw_filter_taps(key, part):
    key_pick, key_fast, key_slow, key_noise, key_tail_len, key_tail = jax.random.split(key, 6)
    fast_share = 0.45
    chooser = jax.random.uniform(key_pick, (CH,), jnp.float32)
    fast_len = jax.random.uniform(key_fast, (CH,), jnp.float32, minval=30.0, maxval=50.0)
    slow_len = 1.0 * LENGTH * jnp.exp(jax.random.uniform(key_slow, (CH,), jnp.float32, minval=math.log(0.5), maxval=math.log(4.0)))
    decay_len = jnp.where(chooser < fast_share, fast_len, slow_len)
    amplitude = jnp.sqrt(1.0 - jnp.exp(-2.0 / decay_len))
    tail_len = 1.0 * LENGTH * jnp.exp(jax.random.uniform(key_tail_len, (CH,), jnp.float32, minval=0.0, maxval=math.log(4.0)))
    tail_amp = 0.4 * jnp.sqrt(1.0 - jnp.exp(-2.0 / tail_len))
    positions = jnp.arange(LENGTH, dtype=jnp.float32)[:, None]
    noise_vals = jnp.clip(jax.random.normal(key_noise, (LENGTH, CH), jnp.float32), -3.5, 3.5)
    tail_noise = jnp.clip(jax.random.normal(key_tail, (LENGTH, CH), jnp.float32), -3.5, 3.5)
    head_part = amplitude * jnp.exp(-positions / decay_len) * noise_vals
    tail_part = tail_amp * jnp.exp(-positions / tail_len) * tail_noise
    return head_part + tail_part


def level_of(key, extent, pieces, smallest, largest):
    def one(dim, shards_of):
        heights = jax.random.uniform(jax.random.fold_in(jax.random.fold_in(key, 6), dim), (shards_of,), jnp.float32, smallest / len(pieces), largest / len(pieces))
        return jnp.repeat(jnp.exp(heights), extent[dim] // shards_of).reshape((-1,) + (1,) * (len(extent) - dim - 1))

    gain = one(*pieces[0])
    for cut in pieces[1:]:
        gain = gain * one(*cut)
    return gain


def bell_draw(own_key, dims, deviation, bound, cuts=(), kind=jnp.bfloat16):
    entries = jax.random.normal(own_key, dims, jnp.float32) * deviation
    if len(cuts) > 0:
        entries = level_of(own_key, dims, cuts, -0.22, 0.18) * entries
    return jnp.clip(entries, min=-bound, max=bound).astype(kind)


def setup_inputs(seed: int = 0) -> dict:
    keys = jax.random.split(jax.random.key(seed), 6)
    return {
        "tokens": bell_draw(keys[0], (LENGTH, D), 1.0, 6.0, ((0, 32), (1, 4))),
        "in_weight": bell_draw(keys[1], (D, 3, CH), D ** -0.5, 0.09375, ((2, 4),)),
        "short_weight": bell_draw(keys[2], (3, 3, CH), 0.6, 3.0, ((2, 4),), jnp.float32),
        "filter_taps": draw_filter_taps(jax.random.fold_in(keys[5], 71), 0),
        "skip_gain": bell_draw(keys[4], (CH,), 1.0, 3.0, ((0, 4),), jnp.float32),
    }


def reference(tokens, in_weight, short_weight, filter_taps, skip_gain):
    projected = jnp.dot(tokens, in_weight.reshape(D, 3 * CH), preferred_element_type=jnp.float32).astype(jnp.bfloat16).reshape(LENGTH, 3, CH)
    proj_f32 = projected.astype(jnp.float32)
    padded = jnp.pad(proj_f32, ((2, 0), (0, 0), (0, 0)))
    shorted = (short_weight[0] * proj_f32 + short_weight[1] * padded[1:-1] + short_weight[2] * padded[:-2]).astype(jnp.bfloat16)
    short_f32 = shorted.astype(jnp.float32)
    mixed_in = short_f32[:, 1] * short_f32[:, 2]
    block_width = min(CH, 256)

    def one_block(block_index):
        first_col = block_index * block_width
        data_block = lax.dynamic_slice_in_dim(mixed_in, first_col, block_width, 1)
        taps_block = lax.dynamic_slice_in_dim(filter_taps, first_col, block_width, 1)
        spectrum = jnp.fft.rfft(data_block, n=2 * LENGTH, axis=0) * jnp.fft.rfft(taps_block, n=2 * LENGTH, axis=0)
        return jnp.fft.irfft(spectrum, n=2 * LENGTH, axis=0)[:LENGTH]

    conv_blocks = lax.map(one_block, jnp.arange(CH // block_width, dtype=jnp.int32))
    conv_vals = jnp.transpose(conv_blocks, (1, 0, 2)).reshape(LENGTH, CH)
    return ((conv_vals + skip_gain * mixed_in) * short_f32[:, 0]).astype(jnp.bfloat16)
```

```python
import jax
import jax.numpy as jnp
import numpy as np
from jax import lax
from jax.sharding import PartitionSpec as P

exact = lax.Precision.HIGHEST
SIDE = 128


def transform_tables():
    n = np.arange(SIDE)
    odd = n + 0.5
    first = -2.0 * np.pi / (2 * SIDE) * np.outer(odd, n)
    turn = -2.0 * np.pi / (2 * SIDE * SIDE) * np.outer(odd, n)
    second = -2.0 * np.pi / SIDE * np.outer(n, n)
    wide = np.concatenate([np.cos(first), np.sin(first)], 0)
    cos2, sin2 = np.cos(second), np.sin(second)
    mix = np.block([[cos2, sin2], [-sin2, cos2]])
    back = np.block([[cos2, -sin2], [sin2, cos2]]) / (SIDE * SIDE)
    return [np.asarray(a, np.float32) for a in (wide, np.cos(turn), np.sin(turn), mix, back)]


def forward(x, tables):
    wide, cosine, sine, mix, _ = tables
    a = jnp.einsum("kn,cnm->ckm", wide, x, precision=exact)
    re, im = a[:, :SIDE], a[:, SIDE:]
    turned = jnp.concatenate([re * cosine - im * sine, re * sine + im * cosine], axis=2)
    b = jnp.einsum("ckm,mf->ckf", turned, mix, precision=exact)
    return b[:, :, :SIDE], b[:, :, SIDE:]


def inverse(re, im, tables):
    wide, cosine, sine, _, back = tables
    c = jnp.einsum("ckf,fm->ckm", jnp.concatenate([re, im], axis=2), back, precision=exact)
    re, im = c[:, :, :SIDE], c[:, :, SIDE:]
    turned = jnp.concatenate([re * cosine + im * sine, im * cosine - re * sine], axis=1)
    return jnp.einsum("kn,ckm->cnm", wide, turned, precision=exact)


def local(tokens, in_weight, short_weight, filter_taps, skip_gain):
    rows, channels = filter_taps.shape
    seq_count = lax.axis_size("seq")
    own = channels // seq_count
    tables = transform_tables()

    def to_channels(values):
        parts = values.astype(jnp.bfloat16).T.reshape(seq_count, own, rows)
        parts = lax.all_to_all(parts, "seq", 0, 0, tiled=True)
        return parts.astype(jnp.float32).transpose(1, 0, 2).reshape(own, SIDE, SIDE)

    filter_re, filter_im = forward(to_channels(filter_taps), tables)
    projected = jnp.einsum(
        "td,dgc->tgc",
        lax.all_gather(tokens, "chan", axis=1, tiled=True),
        in_weight,
        preferred_element_type=jnp.float32,
    ).astype(jnp.bfloat16)
    pairs = [(i, i + 1) for i in range(seq_count - 1)]
    previous = lax.ppermute(projected[rows - 2 :], "seq", pairs)
    extended = jnp.concatenate([previous, projected], axis=0).astype(jnp.float32)
    shorted = (
        short_weight[0] * extended[2:]
        + short_weight[1] * extended[1:-1]
        + short_weight[2] * extended[:-2]
    ).astype(jnp.bfloat16)
    short_f32 = shorted.astype(jnp.float32)
    mixed_in = short_f32[:, 1] * short_f32[:, 2]
    data_re, data_im = forward(to_channels(mixed_in), tables)
    prod_re = data_re * filter_re - data_im * filter_im
    prod_im = data_re * filter_im + data_im * filter_re
    result = inverse(prod_re, prod_im, tables)
    parts = result.reshape(own, seq_count, rows).transpose(1, 0, 2).astype(jnp.bfloat16)
    parts = lax.all_to_all(parts, "seq", 0, 0, tiled=True)
    conv_vals = parts.reshape(channels, rows).T.astype(jnp.float32)
    return ((conv_vals + skip_gain * mixed_in) * short_f32[:, 0]).astype(jnp.bfloat16)


def solution(mesh):
    return jax.shard_map(
        local,
        mesh=mesh,
        in_specs=(
            P("seq", "chan"),
            P(None, None, "chan"),
            P(None, None, "chan"),
            P("seq", "chan"),
            P("chan"),
        ),
        out_specs=P("seq", "chan"),
        check_vma=False,
    )
```
